256 devices in a mesh: mp: 2 (over x_hi), row: 8 (over z), col: 16 (over x_lo, y, core).
Axes of the slice: x: 4 (x_hi: 2, x_lo: 2; x = x_hi * 2 + x_lo), y: 4, z: 8, core: 2. Of those that a mesh axis runs over, the one named last changes fastest.
Arguments:
- gram_tiles: bfloat16 [4, 16, 8, 128, 16384], P('mp', None, 'row', None, 'col'), may hold values from -4 to 64, as said below
- weights: bfloat16 [4, 16384, 128], P('mp', ('col', 'row')), may hold values from -8 to 8
- damping: float32 [128], replicated, may hold values from 0.5 to 4
Outputs:
- merged: float32 [16384, 128], P(('col', 'row'))
- residual: float32 [16384, 128], P(('col', 'row'))
The draws below stay inside these ranges and needn't reach their ends.
Inputs may be any that keep to these rules, and one draw needn't show every extreme that they name: `gram_tiles`: each model's 16384 x 16384 Gram, read as in the first step, is symmetric positive definite.
All inputs are finite; a program needn't handle non-finite values.
Results may differ from the reference program's by a relative error of at most 0.012.
The reference program's roundings to bfloat16 on the way count: a program that leaves them out, or rounds other values in their place, can miss the bound.
Values may be sent and summed in bfloat16 or wider, within the bound.
No kernel may reach another device: no remote copies, remote signals or barrier semaphores. Data moves between devices by JAX's collectives and lax.ppermute only.
A program may use at most 64 MiB of HBM per device.

```python
import math
import jax
import jax.numpy as jnp
from jax import lax

D = 16384
K = 128
ITERS = 2
MODELS = 4
ROW_BLOCKS = 8
COL_BLOCKS = 16
PIECE = 128


def draw_gram_tiles(key, part):
    model_keys = jax.random.split(jax.random.fold_in(key, 11), MODELS)
    block_key = jax.random.fold_in(key, 31)
    order = jax.random.permutation(block_key, ROW_BLOCKS).astype(jnp.float32)
    exponent = -0.5 + order / float(max(ROW_BLOCKS - 1, 1))
    block_values = jnp.exp(exponent * math.log(3.0))
    block_of = jnp.arange(D) // PIECE % ROW_BLOCKS
    block_scale = block_values[block_of]

    def one_model(model_key):
        first_key, second_key = jax.random.split(model_key, 2)
        normal_part = jax.random.truncated_normal(first_key, -4.0, 4.0, (D, D), jnp.float32)
        symmetric = (normal_part + normal_part.T) * (1.0 / math.sqrt(2.0 * D))
        diagonal = jax.random.uniform(second_key, (D,), jnp.float32, 2.5, 6.0)
        positions = jnp.arange(D)
        symmetric = symmetric.at[positions, positions].add(diagonal)
        scales = block_scale
        symmetric = symmetric * scales[:, None] * scales[None, :]
        return symmetric.astype(jnp.bfloat16)
    grams = lax.map(one_model, model_keys)
    return grams.reshape(MODELS, COL_BLOCKS, ROW_BLOCKS, PIECE, D)


def draw_weights(key, part):
    first_key = jax.random.fold_in(jax.random.fold_in(key, 23), 0)
    row_scale = 0.6 + 1.2 * jnp.arange(D, dtype=jnp.float32) / (D - 1)
    values = jax.random.truncated_normal(first_key, -4.0, 4.0, (MODELS, D, K), jnp.float32)
    return (values * row_scale[None, :, None]).astype(jnp.bfloat16)


def setup_inputs(seed: int = 0) -> dict:
    keys = jax.random.split(jax.random.key(seed), 4)
    return {
        "gram_tiles": draw_gram_tiles(jax.random.fold_in(keys[3], 71), 0),
        "weights": draw_weights(jax.random.fold_in(keys[3], 71), 0),
        "damping": jnp.clip(jnp.exp(jax.random.uniform(keys[2], (K,), jnp.float32, math.log(0.5), math.log(4.0))), 0.5, 4.0),
    }


def apply_models(matrices, vectors):
    def add_model(running, operands):
        matrix, vector = operands
        return running + jnp.dot(matrix, vector, preferred_element_type=jnp.float32), None

    initial = jnp.zeros((D, K), jnp.float32)
    running, unused = lax.scan(add_model, initial, (matrices, vectors))
    return running


def reference(gram_tiles, weights, damping):
    matrices = gram_tiles.reshape(MODELS, D, D)
    target = apply_models(matrices, weights)
    merged = jnp.zeros((D, K), jnp.float32)
    residual = target
    direction = target
    norm_now = jnp.sum(residual * residual, axis=0)
    for iteration in range(ITERS):
        low_dir = direction.astype(jnp.bfloat16)
        applied = apply_models(matrices, jnp.broadcast_to(low_dir[None], (MODELS, D, K)))
        dir_wide = low_dir.astype(jnp.float32)
        applied = applied + damping[None, :] * dir_wide
        curve_term = jnp.sum(dir_wide * applied, axis=0)
        step_size = norm_now / curve_term
        merged = merged + step_size[None, :] * direction
        residual = residual - step_size[None, :] * applied
        if iteration + 1 < ITERS:
            norm_next = jnp.sum(residual * residual, axis=0)
            direction = residual + (norm_next / norm_now)[None, :] * direction
            norm_now = norm_next
    return merged, residual
```

```python
import jax
import jax.numpy as jnp
from jax import lax
from jax.sharding import PartitionSpec as P

ITERS = 2
PLANE = ("col", "mp")
LINE = ("row", "mp")


def spread_rows(piece, axes, count):
    copies = jnp.broadcast_to(piece[None], (count,) + piece.shape)
    return lax.all_to_all(copies, axes, 0, 0)


def sum_over(values, axes, count):
    return jnp.sum(spread_rows(values, axes, count), axis=0)


def scatter_sum(partial_value, axes, count):
    rows = partial_value.shape[0] // count
    blocks = partial_value.reshape(count, rows, partial_value.shape[1])
    return jnp.sum(lax.all_to_all(blocks, axes, 0, 0), axis=0)


def multiply(gram_tile, portion):
    spread = jnp.broadcast_to(portion, (gram_tile.shape[0],) + portion.shape[1:])
    return jnp.einsum("mij,mjk->ik", gram_tile, spread, preferred_element_type=jnp.float32)


def make_on_device(sizes):
    mp, row, col = sizes["mp"], sizes["row"], sizes["col"]

    def gather(piece):
        whole = spread_rows(piece, LINE, row * mp)
        return whole.reshape(1, -1, piece.shape[-1])

    def on_device(gram_tiles, weights, damping):
        shape_in = gram_tiles.shape
        gram_tile = gram_tiles.reshape(
            shape_in[0], shape_in[1] * shape_in[2] * shape_in[3], shape_in[4]
        )
        wide = spread_rows(weights, "row", row)
        wide = jnp.swapaxes(wide, 0, 1).reshape(weights.shape[0], -1, weights.shape[2])
        residual = scatter_sum(multiply(gram_tile, wide), PLANE, col * mp)

        low = residual.astype(jnp.bfloat16)
        applied = scatter_sum(multiply(gram_tile, gather(low)), PLANE, col * mp)
        low_wide = low.astype(jnp.float32)
        applied = applied + damping[None, :] * low_wide
        sums = jnp.stack(
            [
                jnp.sum(residual * residual, axis=0),
                jnp.sum(low_wide * applied, axis=0),
                jnp.sum(residual * applied, axis=0),
                jnp.sum(applied * applied, axis=0),
            ]
        )
        sums = sum_over(sum_over(sums, LINE, row * mp), "col", col)
        norm, curve, cross, square = sums[0], sums[1], sums[2], sums[3]
        step = norm / curve
        merged = step[None, :] * residual
        new_residual = residual - step[None, :] * applied
        norm_next = jnp.maximum((norm - step * cross) - step * (cross - step * square), 0.0)
        direction = new_residual + (norm_next / norm)[None, :] * residual

        low = direction.astype(jnp.bfloat16)
        applied = scatter_sum(multiply(gram_tile, gather(low)), PLANE, col * mp)
        low_wide = low.astype(jnp.float32)
        applied = applied + damping[None, :] * low_wide
        curve = jnp.sum(low_wide * applied, axis=0)
        curve = sum_over(curve, ("mp", "row", "col"), mp * row * col)
        step = norm_next / curve
        merged = merged + step[None, :] * direction
        residual = new_residual - step[None, :] * applied

        half = jnp.stack([merged, residual])
        other = lax.ppermute(half, "mp", [(0, 1), (1, 0)])
        mine = lax.axis_index("mp")
        first = jnp.where(mine == 0, half, other)
        second = jnp.where(mine == 0, other, half)
        out = jnp.concatenate([first, second], axis=1)
        return out[0], out[1]

    return on_device


def solution(mesh):
    in_specs = (P("mp", None, "row", None, "col"), P("mp", ("col", "row"), None), P())
    out_specs = (P(("col", "row"), None), P(("col", "row"), None))
    return jax.shard_map(
        make_on_device(dict(mesh.shape)),
        mesh=mesh,
        in_specs=in_specs,
        out_specs=out_specs,
        check_vma=False,
    )
```

```python
import jax
import jax.numpy as jnp
from jax import lax
from jax.experimental import pallas as pl
from jax.experimental.pallas import tpu as pltpu
from jax.sharding import PartitionSpec as P

SWAP = [(0, 1), (1, 0)]
PLANE = ("xlo", "y")
ALL = ("row", "xlo", "y")


def spread(piece, axes, count):
    copies = jnp.broadcast_to(piece[None], (count,) + piece.shape)
    return lax.all_to_all(copies, axes, 0, 0)


def product_kernel(half_ref, gram_ref, portion_ref, out_ref):
    models, steps, _, rows, depth = gram_ref.shape
    total = None
    for model in range(models):
        tile = gram_ref[model].reshape(steps * rows, depth)
        term = jnp.dot(
            tile,
            portion_ref[model % portion_ref.shape[0]],
            preferred_element_type=jnp.float32,
        )
        total = term if total is None else total + term
    out_ref[...] = total.reshape(out_ref.shape)


def half_product(gram, portion, half):
    models, blocks, _, rows, depth = gram.shape
    width = portion.shape[2]
    group = 2
    return pl.pallas_call(
        product_kernel,
        out_shape=jax.ShapeDtypeStruct((blocks, rows, width), jnp.float32),
        grid_spec=pltpu.PrefetchScalarGridSpec(
            num_scalar_prefetch=1,
            grid=(blocks // group,),
            in_specs=[
                pl.BlockSpec(
                    (models, group, 1, rows, depth), lambda i, h: (0, i, h[0], 0, 0)
                ),
                pl.BlockSpec(portion.shape, lambda i, h: (0, 0, 0)),
            ],
            out_specs=pl.BlockSpec((group, rows, width), lambda i, h: (i, 0, 0)),
        ),
        cost_estimate=pl.CostEstimate(
            flops=2 * models * blocks * rows * depth * width,
            bytes_accessed=2 * models * blocks * rows * depth,
            transcendentals=0,
        ),
    )(half, gram, portion)


def make_on_device(sizes):
    row, plane = sizes["row"], sizes["xlo"] * sizes["y"]

    def gather(piece):
        return spread(piece, "row", row).reshape(1, -1, piece.shape[-1])

    def apply_models(gram, portion):
        core = lax.axis_index("core").astype(jnp.int32).reshape(1)
        sent = half_product(gram, portion, 1 - core)
        arrived = lax.ppermute(sent, "core", SWAP)
        kept = half_product(gram, portion, core) + arrived
        piece = jnp.sum(lax.all_to_all(kept, PLANE, 0, 0), axis=0)
        return piece + lax.ppermute(piece, "mp", SWAP)

    def total(values):
        values = values + lax.ppermute(values, "core", SWAP)
        return jnp.sum(spread(values, ALL, row * plane), axis=0)

    def on_device(gram_tiles, weights, damping):
        shape_in = gram_tiles.shape
        gram = gram_tiles.reshape(
            shape_in[0], plane, 2, shape_in[2] * shape_in[3], shape_in[4]
        )
        wide = spread(weights, "row", row)
        wide = jnp.swapaxes(wide, 0, 1).reshape(weights.shape[0], -1, weights.shape[2])
        residual = apply_models(gram, wide)

        low = residual.astype(jnp.bfloat16)
        applied = apply_models(gram, gather(low))
        low_wide = low.astype(jnp.float32)
        applied = applied + damping[None, :] * low_wide
        sums = total(
            jnp.stack(
                [
                    jnp.sum(residual * residual, axis=0),
                    jnp.sum(low_wide * applied, axis=0),
                    jnp.sum(residual * applied, axis=0),
                    jnp.sum(applied * applied, axis=0),
                ]
            )
        )
        norm, curve, cross, square = sums[0], sums[1], sums[2], sums[3]
        step = norm / curve
        merged = step[None, :] * residual
        new_residual = residual - step[None, :] * applied
        norm_next = jnp.maximum((norm - step * cross) - step * (cross - step * square), 0.0)
        direction = new_residual + (norm_next / norm)[None, :] * residual

        low = direction.astype(jnp.bfloat16)
        applied = apply_models(gram, gather(low))
        low_wide = low.astype(jnp.float32)
        applied = applied + damping[None, :] * low_wide
        curve = total(jnp.sum(low_wide * applied, axis=0)[None])[0]
        step = norm_next / curve
        merged = merged + step[None, :] * direction
        residual = new_residual - step[None, :] * applied
        return merged, residual

    return on_device


def solution(mesh):
    shape = (mesh.shape["mp"], mesh.shape["row"], mesh.shape["col"] // 8, 4, 2)
    fine = jax.sharding.Mesh(
        mesh.devices.reshape(shape), ("mp", "row", "xlo", "y", "core")
    )
    col = ("xlo", "y", "core")
    in_specs = (P("mp", None, "row", None, col), P("mp", col + ("row",), None), P())
    out_specs = (P(col + ("row",), None), P(col + ("row",), None))
    return jax.shard_map(
        make_on_device(dict(fine.shape)),
        mesh=fine,
        in_specs=in_specs,
        out_specs=out_specs,
        check_vma=False,
    )
```

```python
import functools

import jax
import jax.numpy as jnp
from jax import lax
from jax.experimental import pallas as pl
from jax.experimental.pallas import tpu as pltpu
from jax.sharding import PartitionSpec as P

SMALL = 12 * 2**20
SWAP = [(0, 1), (1, 0)]
PLANE = ("xlo", "y")
ONE_GROUP = ("row", "xlo", "y")
BOTH_GROUPS = ("mp", "row", "xlo", "y")


def spread(piece, axes, count):
    copies = jnp.broadcast_to(piece[None], (count,) + piece.shape)
    return lax.all_to_all(copies, axes, 0, 0)


def product_kernel(own, gram_ref, portion_ref, out_ref):
    models, blocks, _, rows, depth = gram_ref.shape
    core = lax.axis_index("core")
    half = core if own else 1 - core
    total = None
    for model in range(models):
        tile = gram_ref[model, :, half].reshape(blocks * rows, depth)
        portion = portion_ref[:, model % portion_ref.shape[1]].reshape(depth, -1)
        term = jnp.dot(tile, portion, preferred_element_type=jnp.float32)
        total = term if total is None else total + term
    out_ref[...] = total.reshape(out_ref.shape)


def half_product(gram, portion, own):
    models, blocks, _, rows, depth = gram.shape
    width = portion.shape[3]
    return pl.pallas_call(
        functools.partial(product_kernel, own),
        out_shape=jax.ShapeDtypeStruct((blocks, rows, width), jnp.float32),
        in_specs=[pl.BlockSpec(memory_space=pltpu.VMEM)] * 2,
        out_specs=pl.BlockSpec(memory_space=pltpu.VMEM),
        compiler_params=pltpu.CompilerParams(vmem_limit_bytes=SMALL),
        cost_estimate=pl.CostEstimate(
            flops=2 * models * blocks * rows * depth * width,
            bytes_accessed=2 * models * blocks * rows * depth,
            transcendentals=0,
        ),
    )(gram, portion)


def sum_kernel(values_ref, out_ref):
    out_ref[...] = jnp.sum(values_ref[...], axis=0)


def sum_leading(values):
    return pl.pallas_call(
        sum_kernel,
        out_shape=jax.ShapeDtypeStruct(values.shape[1:], values.dtype),
        in_specs=[pl.BlockSpec(memory_space=pltpu.VMEM)],
        out_specs=pl.BlockSpec(memory_space=pltpu.VMEM),
        compiler_params=pltpu.CompilerParams(vmem_limit_bytes=SMALL),
        cost_estimate=pl.CostEstimate(
            flops=values.size, bytes_accessed=4 * values.size, transcendentals=0
        ),
    )(values)


def make_on_device(sizes):
    row, plane = sizes["row"], sizes["xlo"] * sizes["y"]

    def gather(piece):
        return spread(piece, "row", row)[:, None]

    def apply_models(gram, portion):
        sent = half_product(gram, portion, False)
        arrived = lax.ppermute(sent, "core", SWAP)
        kept = half_product(gram, portion, True) + arrived
        return sum_leading(lax.all_to_all(kept, PLANE, 0, 0))

    def over_mp(piece):
        return piece + lax.ppermute(piece, "mp", SWAP)

    def total(values, axes):
        values = values + lax.ppermute(values, "core", SWAP)
        count = 1
        for axis in axes:
            count = count * sizes[axis]
        return sum_leading(spread(values, axes, count))

    def on_device(gram_tiles, weights, damping):
        shape_in = gram_tiles.shape
        gram = gram_tiles.reshape(
            shape_in[0], plane, 2, shape_in[2] * shape_in[3], shape_in[4]
        )
        residual = over_mp(apply_models(gram, spread(weights, "row", row)))

        low = residual.astype(jnp.bfloat16)
        applied = over_mp(apply_models(gram, gather(low)))
        low_wide = low.astype(jnp.float32)
        applied = applied + damping[None, :] * low_wide
        sums = total(
            jnp.stack(
                [
                    jnp.sum(residual * residual, axis=0),
                    jnp.sum(low_wide * applied, axis=0),
                    jnp.sum(residual * applied, axis=0),
                    jnp.sum(applied * applied, axis=0),
                ]
            ),
            ONE_GROUP,
        )
        norm, curve, cross, square = sums[0], sums[1], sums[2], sums[3]
        step = norm / curve
        merged = step[None, :] * residual
        new_residual = residual - step[None, :] * applied
        norm_next = jnp.maximum((norm - step * cross) - step * (cross - step * square), 0.0)
        direction = new_residual + (norm_next / norm)[None, :] * residual

        low = direction.astype(jnp.bfloat16)
        share = apply_models(gram, gather(low))
        applied = over_mp(share)
        low_wide = low.astype(jnp.float32)
        applied = applied + damping[None, :] * low_wide
        share = share + (0.5 * damping)[None, :] * low_wide
        curve = total(jnp.sum(low_wide * share, axis=0)[None], BOTH_GROUPS)[0]
        step = norm_next / curve
        merged = merged + step[None, :] * direction
        residual = new_residual - step[None, :] * applied
        return merged, residual

    return on_device


def solution(mesh):
    shape = (mesh.shape["mp"], mesh.shape["row"], mesh.shape["col"] // 8, 4, 2)
    fine = jax.sharding.Mesh(
        mesh.devices.reshape(shape), ("mp", "row", "xlo", "y", "core")
    )
    col = ("xlo", "y", "core")
    in_specs = (P("mp", None, "row", None, col), P("mp", col + ("row",), None), P())
    out_specs = (P(col + ("row",), None), P(col + ("row",), None))
    return jax.shard_map(
        make_on_device(dict(fine.shape)),
        mesh=fine,
        in_specs=in_specs,
        out_specs=out_specs,
        check_vma=False,
    )
```

```python
import functools

import jax
import jax.numpy as jnp
from jax import lax
from jax.experimental import pallas as pl
from jax.experimental.pallas import tpu as pltpu
from jax.sharding import PartitionSpec as P


LARGE = 50 * 2**20
SMALL = 12 * 2**20
SWAP = [(0, 1), (1, 0)]
PLANE = ("xlo", "y")
ONE_GROUP = ("row", "xlo", "y")
BOTH_GROUPS = ("mp", "row", "xlo", "y")


def spread(piece, axes, count):
    copies = jnp.broadcast_to(piece[None], (count,) + piece.shape)
    return lax.all_to_all(copies, axes, 0, 0)


def product_kernel(own, gram_ref, portion_ref, out_ref):
    models, blocks, _, rows, depth = gram_ref.shape
    core = lax.axis_index("core")
    half = core if own else 1 - core
    total = None
    for model in range(models):
        tile = gram_ref[model, :, half].reshape(blocks * rows, depth)
        portion = portion_ref[:, model % portion_ref.shape[1]].reshape(depth, -1)
        term = jnp.dot(tile, portion, preferred_element_type=jnp.float32)
        total = term if total is None else total + term
    out_ref[...] = total.reshape(out_ref.shape)


def half_product(gram, portion, own):
    models, blocks, _, rows, depth = gram.shape
    width = portion.shape[3]
    return pl.pallas_call(
        functools.partial(product_kernel, own),
        out_shape=jax.ShapeDtypeStruct((blocks, rows, width), jnp.float32),
        in_specs=[pl.BlockSpec(memory_space=pltpu.VMEM)] * 2,
        out_specs=pl.BlockSpec(memory_space=pltpu.VMEM),
        compiler_params=pltpu.CompilerParams(vmem_limit_bytes=SMALL),
        cost_estimate=pl.CostEstimate(
            flops=2 * models * blocks * rows * depth * width,
            bytes_accessed=2 * models * blocks * rows * depth,
            transcendentals=0,
        ),
    )(gram, portion)


def sum_kernel(values_ref, out_ref):
    out_ref[...] = jnp.sum(values_ref[...], axis=0)


def sum_leading(values):
    return pl.pallas_call(
        sum_kernel,
        out_shape=jax.ShapeDtypeStruct(values.shape[1:], values.dtype),
        in_specs=[pl.BlockSpec(memory_space=pltpu.VMEM)],
        out_specs=pl.BlockSpec(memory_space=pltpu.VMEM),
        compiler_params=pltpu.CompilerParams(vmem_limit_bytes=SMALL),
        cost_estimate=pl.CostEstimate(
            flops=values.size, bytes_accessed=4 * values.size, transcendentals=0
        ),
    )(values)


def streamed_kernel(own, gram_ref, portion_ref, out_ref, tiles, arrived):
    models, blocks, _, _, depth = gram_ref.shape
    core = lax.axis_index("core")
    half = core if own else 1 - core
    copies = [
        pltpu.make_async_copy(gram_ref.at[:, block, half], tiles.at[block], arrived.at[block])
        for block in range(blocks)
    ]
    for copy in copies:
        copy.start()
    for block in range(blocks):
        copies[block].wait()
        total = None
        for model in range(models):
            portion = portion_ref[:, model].reshape(depth, -1)
            term = jnp.dot(tiles[block, model], portion, preferred_element_type=jnp.float32)
            total = term if total is None else total + term
        out_ref[block] = total


def half_product_streamed(gram, portion, own):
    models, blocks, _, rows, depth = gram.shape
    width = portion.shape[3]
    return pl.pallas_call(
        functools.partial(streamed_kernel, own),
        out_shape=jax.ShapeDtypeStruct((blocks, rows, width), jnp.float32),
        in_specs=[
            pl.BlockSpec(memory_space=pltpu.HBM),
            pl.BlockSpec(memory_space=pltpu.VMEM),
        ],
        out_specs=pl.BlockSpec(memory_space=pltpu.VMEM),
        scratch_shapes=[
            pltpu.VMEM((blocks, models, rows, depth), gram.dtype),
            pltpu.SemaphoreType.DMA((blocks,)),
        ],
        compiler_params=pltpu.CompilerParams(vmem_limit_bytes=LARGE),
        cost_estimate=pl.CostEstimate(
            flops=2 * models * blocks * rows * depth * width,
            bytes_accessed=2 * models * blocks * rows * depth,
            transcendentals=0,
        ),
    )(gram, portion)


def last_kernel(values_ref, low_ref, damping_ref, share_ref, curve_ref):
    share = jnp.sum(values_ref[...], axis=0)
    low = low_ref[...].astype(jnp.float32)
    damped = share + (0.5 * damping_ref[...]) * low
    share_ref[...] = share
    curve_ref[...] = jnp.sum(low * damped, axis=0, keepdims=True)


def last_sums(values, low, damping):
    rows, width = low.shape
    return pl.pallas_call(
        last_kernel,
        out_shape=(
            jax.ShapeDtypeStruct((rows, width), jnp.float32),
            jax.ShapeDtypeStruct((1, width), jnp.float32),
        ),
        in_specs=[pl.BlockSpec(memory_space=pltpu.VMEM)] * 3,
        out_specs=(pl.BlockSpec(memory_space=pltpu.VMEM),) * 2,
        compiler_params=pltpu.CompilerParams(vmem_limit_bytes=SMALL),
        cost_estimate=pl.CostEstimate(
            flops=values.size, bytes_accessed=4 * values.size, transcendentals=0
        ),
    )(values, low, damping)


def make_on_device(sizes):
    row, plane = sizes["row"], sizes["xlo"] * sizes["y"]

    def gather(piece):
        return spread(piece, "row", row)[:, None]

    def apply_models(gram, portion, product=half_product):
        sent = product(gram, portion, False)
        arrived = lax.ppermute(sent, "core", SWAP)
        kept = product(gram, portion, True) + arrived
        return lax.all_to_all(kept, PLANE, 0, 0)

    def over_mp(blocks):
        piece = sum_leading(blocks)
        return piece + lax.ppermute(piece, "mp", SWAP)

    def total(values, axes):
        values = values + lax.ppermute(values, "core", SWAP)
        count = 1
        for axis in axes:
            count = count * sizes[axis]
        return sum_leading(spread(values, axes, count))

    def on_device(gram_tiles, weights, damping):
        shape_in = gram_tiles.shape
        gram = gram_tiles.reshape(
            shape_in[0], plane, 2, shape_in[2] * shape_in[3], shape_in[4]
        )
        residual = over_mp(
            apply_models(gram, spread(weights, "row", row), half_product_streamed)
        )

        low = residual.astype(jnp.bfloat16)
        applied = over_mp(apply_models(gram, gather(low)))
        low_wide = low.astype(jnp.float32)
        applied = applied + damping[None, :] * low_wide
        sums = total(
            jnp.stack(
                [
                    jnp.sum(residual * residual, axis=0),
                    jnp.sum(low_wide * applied, axis=0),
                    jnp.sum(residual * applied, axis=0),
                    jnp.sum(applied * applied, axis=0),
                ]
            ),
            ONE_GROUP,
        )
        norm, curve, cross, square = sums[0], sums[1], sums[2], sums[3]
        step = norm / curve
        merged = step[None, :] * residual
        new_residual = residual - step[None, :] * applied
        norm_next = jnp.maximum((norm - step * cross) - step * (cross - step * square), 0.0)
        direction = new_residual + (norm_next / norm)[None, :] * residual

        low = direction.astype(jnp.bfloat16)
        share, curve = last_sums(apply_models(gram, gather(low)), low, damping[None, :])
        other = lax.ppermute(share, "mp", SWAP)
        curve = total(curve, BOTH_GROUPS)[0]
        applied = share + other + damping[None, :] * low.astype(jnp.float32)
        step = norm_next / curve
        merged = merged + step[None, :] * direction
        residual = new_residual - step[None, :] * applied
        return merged, residual

    return on_device


def solution(mesh):
    shape = (mesh.shape["mp"], mesh.shape["row"], mesh.shape["col"] // 8, 4, 2)
    fine = jax.sharding.Mesh(
        mesh.devices.reshape(shape), ("mp", "row", "xlo", "y", "core")
    )
    col = ("xlo", "y", "core")
    in_specs = (P("mp", None, "row", None, col), P("mp", col + ("row",), None), P())
    out_specs = (P(col + ("row",), None), P(col + ("row",), None))
    return jax.shard_map(
        make_on_device(dict(fine.shape)),
        mesh=fine,
        in_specs=in_specs,
        out_specs=out_specs,
        check_vma=False,
    )
```

```python
import functools

import jax
import jax.numpy as jnp
from jax import lax
from jax.experimental import pallas as pl
from jax.experimental.pallas import tpu as pltpu
from jax.sharding import PartitionSpec as P

SMALL = 12 * 2**20
SWAP = [(0, 1), (1, 0)]
PLANE = ("xlo", "y")
LINE = ("zhi", "zlo")
ONE_GROUP = LINE + PLANE
BOTH_GROUPS = ("mp",) + LINE + PLANE


def spread(piece, axes, count):
    copies = jnp.broadcast_to(piece[None], (count,) + piece.shape)
    return lax.all_to_all(copies, axes, 0, 0)


def product_kernel(own, gram_ref, portion_ref, out_ref):
    models, blocks, _, rows, depth = gram_ref.shape
    core = lax.axis_index("core")
    half = core if own else 1 - core
    total = None
    for model in range(models):
        tile = gram_ref[model, :, half].reshape(blocks * rows, depth)
        portion = portion_ref[:, model % portion_ref.shape[1]].reshape(depth, -1)
        term = jnp.dot(tile, portion, preferred_element_type=jnp.float32)
        total = term if total is None else total + term
    out_ref[...] = total.reshape(out_ref.shape)


def half_product(gram, portion, own):
    models, blocks, _, rows, depth = gram.shape
    width = portion.shape[3]
    return pl.pallas_call(
        functools.partial(product_kernel, own),
        out_shape=jax.ShapeDtypeStruct((blocks, rows, width), jnp.float32),
        in_specs=[pl.BlockSpec(memory_space=pltpu.VMEM)] * 2,
        out_specs=pl.BlockSpec(memory_space=pltpu.VMEM),
        compiler_params=pltpu.CompilerParams(vmem_limit_bytes=SMALL),
        cost_estimate=pl.CostEstimate(
            flops=2 * models * blocks * rows * depth * width,
            bytes_accessed=2 * models * blocks * rows * depth,
            transcendentals=0,
        ),
    )(gram, portion)


def part_kernel(near, halves, gram_ref, pieces_ref, *refs):
    outs, sums = refs[-len(halves) :], refs[: -len(halves)]
    models, blocks, _, rows, depth = gram_ref.shape
    core, place = lax.axis_index("core"), lax.axis_index("zlo")
    first = place if near else 1 - place
    for slot, own in enumerate(halves):
        half = core if own else 1 - core
        total = None
        for index in range(pieces_ref.shape[0]):
            start = pl.multiple_of((2 * index + first) * rows, rows)
            for model in range(models):
                tile = gram_ref[model, :, half, :, pl.ds(start, rows)]
                term = jnp.dot(
                    tile.reshape(blocks * rows, rows),
                    pieces_ref[index, model],
                    preferred_element_type=jnp.float32,
                )
                total = term if total is None else total + term
        total = total.reshape(outs[slot].shape)
        if sums:
            total = total + sums[slot][...]
        outs[slot][...] = total


def part_product(gram, pieces, near, halves, sums=()):
    models, blocks, _, rows, depth = gram.shape
    width = pieces.shape[3]
    shape = jax.ShapeDtypeStruct((blocks, rows, width), jnp.float32)
    work = len(halves) * pieces.shape[0] * models * blocks * rows * rows
    return pl.pallas_call(
        functools.partial(part_kernel, near, halves),
        out_shape=(shape,) * len(halves),
        in_specs=[pl.BlockSpec(memory_space=pltpu.VMEM)] * (2 + len(sums)),
        out_specs=(pl.BlockSpec(memory_space=pltpu.VMEM),) * len(halves),
        input_output_aliases={2 + slot: slot for slot in range(len(sums))},
        compiler_params=pltpu.CompilerParams(vmem_limit_bytes=SMALL),
        cost_estimate=pl.CostEstimate(
            flops=2 * work * width, bytes_accessed=2 * work, transcendentals=0
        ),
    )(gram, pieces, *sums)


def sum_kernel(values_ref, out_ref):
    out_ref[...] = jnp.sum(values_ref[...], axis=0)


def sum_leading(values):
    return pl.pallas_call(
        sum_kernel,
        out_shape=jax.ShapeDtypeStruct(values.shape[1:], values.dtype),
        in_specs=[pl.BlockSpec(memory_space=pltpu.VMEM)],
        out_specs=pl.BlockSpec(memory_space=pltpu.VMEM),
        compiler_params=pltpu.CompilerParams(vmem_limit_bytes=SMALL),
        cost_estimate=pl.CostEstimate(
            flops=values.size, bytes_accessed=4 * values.size, transcendentals=0
        ),
    )(values)


def last_kernel(values_ref, low_ref, damping_ref, share_ref, curve_ref):
    share = jnp.sum(values_ref[...], axis=0)
    low = low_ref[...].astype(jnp.float32)
    damped = share + (0.5 * damping_ref[...]) * low
    share_ref[...] = share
    curve_ref[...] = jnp.sum(low * damped, axis=0, keepdims=True)


def last_sums(values, low, damping):
    rows, width = low.shape
    return pl.pallas_call(
        last_kernel,
        out_shape=(
            jax.ShapeDtypeStruct((rows, width), jnp.float32),
            jax.ShapeDtypeStruct((1, width), jnp.float32),
        ),
        in_specs=[pl.BlockSpec(memory_space=pltpu.VMEM)] * 3,
        out_specs=(pl.BlockSpec(memory_space=pltpu.VMEM),) * 2,
        compiler_params=pltpu.CompilerParams(vmem_limit_bytes=SMALL),
        cost_estimate=pl.CostEstimate(
            flops=values.size, bytes_accessed=4 * values.size, transcendentals=0
        ),
    )(values, low, damping)


def make_on_device(sizes):
    row, plane = sizes["zhi"] * sizes["zlo"], sizes["xlo"] * sizes["y"]

    def gather(piece):
        return spread(piece, LINE, row)[:, None]

    def apply_models(gram, portion):
        arrived = lax.ppermute(half_product(gram, portion, False), "core", SWAP)
        kept = half_product(gram, portion, True) + arrived
        return lax.all_to_all(kept, PLANE, 0, 0)

    def apply_in_parts(gram, piece):
        near = spread(piece, "zhi", sizes["zhi"])
        far = lax.ppermute(near, "zlo", SWAP)
        sums = part_product(gram, near, True, (False, True))
        (sent,) = part_product(gram, far, False, (False,), sums[:1])
        arrived = lax.ppermute(sent, "core", SWAP)
        (kept,) = part_product(gram, far, False, (True,), sums[1:])
        return lax.all_to_all(kept + arrived, PLANE, 0, 0)

    def over_mp(blocks):
        piece = sum_leading(blocks)
        return piece + lax.ppermute(piece, "mp", SWAP)

    def total(values, axes):
        values = values + lax.ppermute(values, "core", SWAP)
        count = 1
        for axis in axes:
            count = count * sizes[axis]
        return sum_leading(spread(values, axes, count))

    def on_device(gram_tiles, weights, damping):
        shape_in = gram_tiles.shape
        gram = gram_tiles.reshape(
            shape_in[0], plane, 2, shape_in[2] * shape_in[3], shape_in[4]
        )
        residual = over_mp(apply_in_parts(gram, weights))

        low = residual.astype(jnp.bfloat16)
        applied = over_mp(apply_models(gram, gather(low)))
        low_wide = low.astype(jnp.float32)
        applied = applied + damping[None, :] * low_wide
        sums = total(
            jnp.stack(
                [
                    jnp.sum(residual * residual, axis=0),
                    jnp.sum(low_wide * applied, axis=0),
                    jnp.sum(residual * applied, axis=0),
                    jnp.sum(applied * applied, axis=0),
                ]
            ),
            ONE_GROUP,
        )
        norm, curve, cross, square = sums[0], sums[1], sums[2], sums[3]
        step = norm / curve
        merged = step[None, :] * residual
        new_residual = residual - step[None, :] * applied
        norm_next = jnp.maximum((norm - step * cross) - step * (cross - step * square), 0.0)
        direction = new_residual + (norm_next / norm)[None, :] * residual

        low = direction.astype(jnp.bfloat16)
        share, curve = last_sums(apply_models(gram, gather(low)), low, damping[None, :])
        other = lax.ppermute(share, "mp", SWAP)
        curve = total(curve, BOTH_GROUPS)[0]
        applied = share + other + damping[None, :] * low.astype(jnp.float32)
        step = norm_next / curve
        merged = merged + step[None, :] * direction
        residual = new_residual - step[None, :] * applied
        return merged, residual

    return on_device


def solution(mesh):
    shape = (mesh.shape["mp"], mesh.shape["row"] // 2, 2, mesh.shape["col"] // 8, 4, 2)
    fine = jax.sharding.Mesh(
        mesh.devices.reshape(shape), ("mp", "zhi", "zlo", "xlo", "y", "core")
    )
    col = ("xlo", "y", "core")
    in_specs = (P("mp", None, LINE, None, col), P("mp", col + LINE, None), P())
    out_specs = (P(col + LINE, None), P(col + LINE, None))
    return jax.shard_map(
        make_on_device(dict(fine.shape)),
        mesh=fine,
        in_specs=in_specs,
        out_specs=out_specs,
        check_vma=False,
    )
```

```python
import functools

import jax
import jax.numpy as jnp
from jax import lax
from jax.experimental import pallas as pl
from jax.experimental.pallas import tpu as pltpu
from jax.sharding import PartitionSpec as P

SMALL = 12 * 2**20
SWAP = [(0, 1), (1, 0)]
PLANE = ("xlo", "y")
LINE = ("zhi", "zlo")
ONE_GROUP = LINE + PLANE
BOTH_GROUPS = ("mp",) + LINE + PLANE


def spread(piece, axes, count):
    copies = jnp.broadcast_to(piece[None], (count,) + piece.shape)
    return lax.all_to_all(copies, axes, 0, 0)


def product_kernel(own, gram_ref, portion_ref, out_ref):
    models, blocks, _, rows, depth = gram_ref.shape
    core = lax.axis_index("core")
    half = core if own else 1 - core
    total = None
    for model in range(models):
        tile = gram_ref[model, :, half].reshape(blocks * rows, depth)
        portion = portion_ref[:, model % portion_ref.shape[1]].reshape(depth, -1)
        term = jnp.dot(tile, portion, preferred_element_type=jnp.float32)
        total = term if total is None else total + term
    out_ref[...] = total.reshape(out_ref.shape)


def half_product(gram, portion, own):
    models, blocks, _, rows, depth = gram.shape
    width = portion.shape[3]
    return pl.pallas_call(
        functools.partial(product_kernel, own),
        out_shape=jax.ShapeDtypeStruct((blocks, rows, width), jnp.float32),
        in_specs=[pl.BlockSpec(memory_space=pltpu.VMEM)] * 2,
        out_specs=pl.BlockSpec(memory_space=pltpu.VMEM),
        compiler_params=pltpu.CompilerParams(vmem_limit_bytes=SMALL),
        cost_estimate=pl.CostEstimate(
            flops=2 * models * blocks * rows * depth * width,
            bytes_accessed=2 * models * blocks * rows * depth,
            transcendentals=0,
        ),
    )(gram, portion)


def part_kernel(near, halves, gram_ref, pieces_ref, *refs):
    outs, sums = refs[-len(halves) :], refs[: -len(halves)]
    models, blocks, _, rows, depth = gram_ref.shape
    core, place, high = (lax.axis_index(axis) for axis in ("core", "zlo", "zhi"))
    first = place if near else 1 - place
    count = pieces_ref.shape[0]
    for slot, own in enumerate(halves):
        half = core if own else 1 - core
        total = None
        for index in range(count):
            owner = lax.rem(high + (count - index), count)
            start = pl.multiple_of((2 * owner + first) * rows, rows)
            for model in range(models):
                tile = gram_ref[model, :, half, :, pl.ds(start, rows)]
                term = jnp.dot(
                    tile.reshape(blocks * rows, rows),
                    pieces_ref[index, model % pieces_ref.shape[1]],
                    preferred_element_type=jnp.float32,
                )
                total = term if total is None else total + term
        total = total.reshape(outs[slot].shape)
        if sums:
            total = total + sums[slot][...]
        outs[slot][...] = total


def part_product(gram, pieces, near, halves, sums=()):
    models, blocks, _, rows, depth = gram.shape
    width = pieces.shape[3]
    shape = jax.ShapeDtypeStruct((blocks, rows, width), jnp.float32)
    work = len(halves) * pieces.shape[0] * models * blocks * rows * rows
    return pl.pallas_call(
        functools.partial(part_kernel, near, halves),
        out_shape=(shape,) * len(halves),
        in_specs=[pl.BlockSpec(memory_space=pltpu.VMEM)] * (2 + len(sums)),
        out_specs=(pl.BlockSpec(memory_space=pltpu.VMEM),) * len(halves),
        input_output_aliases={2 + slot: slot for slot in range(len(sums))},
        compiler_params=pltpu.CompilerParams(vmem_limit_bytes=SMALL),
        cost_estimate=pl.CostEstimate(
            flops=2 * work * width, bytes_accessed=2 * work, transcendentals=0
        ),
    )(gram, pieces, *sums)


def sum_kernel(values_ref, out_ref):
    out_ref[...] = jnp.sum(values_ref[...], axis=0)


def sum_leading(values):
    return pl.pallas_call(
        sum_kernel,
        out_shape=jax.ShapeDtypeStruct(values.shape[1:], values.dtype),
        in_specs=[pl.BlockSpec(memory_space=pltpu.VMEM)],
        out_specs=pl.BlockSpec(memory_space=pltpu.VMEM),
        compiler_params=pltpu.CompilerParams(vmem_limit_bytes=SMALL),
        cost_estimate=pl.CostEstimate(
            flops=values.size, bytes_accessed=4 * values.size, transcendentals=0
        ),
    )(values)


def last_kernel(values_ref, low_ref, damping_ref, share_ref, curve_ref):
    share = jnp.sum(values_ref[...], axis=0)
    low = low_ref[...].astype(jnp.float32)
    damped = share + (0.5 * damping_ref[...]) * low
    share_ref[...] = share
    curve_ref[...] = jnp.sum(low * damped, axis=0, keepdims=True)


def last_sums(values, low, damping):
    rows, width = low.shape
    return pl.pallas_call(
        last_kernel,
        out_shape=(
            jax.ShapeDtypeStruct((rows, width), jnp.float32),
            jax.ShapeDtypeStruct((1, width), jnp.float32),
        ),
        in_specs=[pl.BlockSpec(memory_space=pltpu.VMEM)] * 3,
        out_specs=(pl.BlockSpec(memory_space=pltpu.VMEM),) * 2,
        compiler_params=pltpu.CompilerParams(vmem_limit_bytes=SMALL),
        cost_estimate=pl.CostEstimate(
            flops=values.size, bytes_accessed=4 * values.size, transcendentals=0
        ),
    )(values, low, damping)


def make_on_device(sizes):
    row, plane = sizes["zhi"] * sizes["zlo"], sizes["xlo"] * sizes["y"]

    def gather(piece):
        return spread(piece, LINE, row)[:, None]

    def apply_models(gram, portion):
        arrived = lax.ppermute(half_product(gram, portion, False), "core", SWAP)
        kept = half_product(gram, portion, True) + arrived
        return lax.all_to_all(kept, PLANE, 0, 0)

    def apply_in_parts(gram, piece):
        count = sizes["zhi"]
        near = jnp.stack(
            [piece]
            + [
                lax.ppermute(piece, "zhi", [(i, (i + hop) % count) for i in range(count)])
                for hop in range(1, count)
            ]
        )
        far = lax.ppermute(near, "zlo", SWAP)
        sums = part_product(gram, near, True, (False, True))
        (sent,) = part_product(gram, far, False, (False,), sums[:1])
        arrived = lax.ppermute(sent, "core", SWAP)
        (kept,) = part_product(gram, far, False, (True,), sums[1:])
        return lax.all_to_all(kept + arrived, PLANE, 0, 0)

    def over_mp(blocks):
        piece = sum_leading(blocks)
        return piece + lax.ppermute(piece, "mp", SWAP)

    def total(values, axes):
        values = values + lax.ppermute(values, "core", SWAP)
        count = 1
        for axis in axes:
            count = count * sizes[axis]
        return sum_leading(spread(values, axes, count))

    def on_device(gram_tiles, weights, damping):
        shape_in = gram_tiles.shape
        gram = gram_tiles.reshape(
            shape_in[0], plane, 2, shape_in[2] * shape_in[3], shape_in[4]
        )
        residual = over_mp(apply_in_parts(gram, weights))

        low = residual.astype(jnp.bfloat16)
        applied = over_mp(apply_models(gram, gather(low)))
        low_wide = low.astype(jnp.float32)
        applied = applied + damping[None, :] * low_wide
        sums = total(
            jnp.stack(
                [
                    jnp.sum(residual * residual, axis=0),
                    jnp.sum(low_wide * applied, axis=0),
                    jnp.sum(residual * applied, axis=0),
                    jnp.sum(applied * applied, axis=0),
                ]
            ),
            ONE_GROUP,
        )
        norm, curve, cross, square = sums[0], sums[1], sums[2], sums[3]
        step = norm / curve
        merged = step[None, :] * residual
        new_residual = residual - step[None, :] * applied
        norm_next = jnp.maximum((norm - step * cross) - step * (cross - step * square), 0.0)
        direction = new_residual + (norm_next / norm)[None, :] * residual

        low = direction.astype(jnp.bfloat16)
        share, curve = last_sums(apply_models(gram, gather(low)), low, damping[None, :])
        other = lax.ppermute(share, "mp", SWAP)
        curve = total(curve, BOTH_GROUPS)[0]
        applied = share + other + damping[None, :] * low.astype(jnp.float32)
        step = norm_next / curve
        merged = merged + step[None, :] * direction
        residual = new_residual - step[None, :] * applied
        return merged, residual

    return on_device


def solution(mesh):
    shape = (mesh.shape["mp"], mesh.shape["row"] // 2, 2, mesh.shape["col"] // 8, 4, 2)
    fine = jax.sharding.Mesh(
        mesh.devices.reshape(shape), ("mp", "zhi", "zlo", "xlo", "y", "core")
    )
    col = ("xlo", "y", "core")
    in_specs = (P("mp", None, LINE, None, col), P("mp", col + LINE, None), P())
    out_specs = (P(col + LINE, None), P(col + LINE, None))
    return jax.shard_map(
        make_on_device(dict(fine.shape)),
        mesh=fine,
        in_specs=in_specs,
        out_specs=out_specs,
        check_vma=False,
    )
```
